32 devices in a mesh: dp: 4 (over y, x), ep: 4 (over z), tp: 2 (over core).
Axes of the slice: x: 2, y: 2, z: 4, core: 2. Of those that a mesh axis runs over, the one named last changes fastest.
Arguments:
- tokens: bfloat16 [2048, 2048], P(('dp', 'ep')), may hold values from -6 to 6
- routes: int32 [2048, 1], P(('dp', 'ep')), may hold values from 0 to 3; in each aligned block of 128 rows (0 to 127, 128 to 255, ...) at most 64 rows name the same one
- gate_weight: bfloat16 [4, 2048, 768], P('ep', None, 'tp'), may hold values from -0.125 to 0.125
- up_weight: bfloat16 [4, 2048, 768], P('ep', None, 'tp'), may hold values from -0.125 to 0.125
- down_weight: bfloat16 [4, 768, 2048], P('ep', 'tp'), may hold values from -0.21875 to 0.21875
- cotangent: bfloat16 [4, 1024, 2048], P('ep', 'dp'), may hold values from -6 to 6
Outputs:
- expert_out: bfloat16 [4, 1024, 2048], P('ep', 'dp', 'tp')
- slots_grad: bfloat16 [4, 1024, 2048], P('ep', 'dp', 'tp')
- grad_gate: float32 [4, 2048, 768], P('ep', 'dp', 'tp')
- grad_up: float32 [4, 2048, 768], P('ep', 'dp', 'tp')
- grad_down: float32 [4, 768, 2048], P('ep', 'tp', 'dp')
The draws below stay inside these ranges and needn't reach their ends.
Inputs may be any that keep to these rules, and one draw needn't show every extreme that they name: `routes`: among the 128 rows of one device (an aligned block), no expert is named by more than 64 rows, a bound that some block reaches.
All inputs are finite; a program needn't handle non-finite values.
Results may differ from the reference program's by a relative error of at most 0.014.
Values may be sent and summed in bfloat16 or wider, within the bound.
No kernel may reach another device: no remote copies, remote signals or barrier semaphores. Data moves between devices by JAX's collectives and lax.ppermute only.
A program may use at most 64 MiB of HBM per device.

```python
import math
import jax
import jax.numpy as jnp
import numpy as np
from jax import lax

MODEL_WIDTH = 2048
HIDDEN_UNITS = 768
GROUP_TOKENS = 128
TOKEN_EXPERTS = 1
ACTIVE_EXPERTS = 4
EXPERT_SLOTS = 64
EXPERT_ROWS = 1024
TOKEN_TOTAL = 2048
N_DP = 4
N_EP = 4


def with_spikes(drawn, stream_key, source, target, parts, factor):
    def block_of(dim):
        return (jnp.arange(drawn.shape[dim]) // (drawn.shape[dim] // parts)).reshape((-1,) + (1,) * (drawn.ndim - 1 - dim))

    near = jax.random.permutation(stream_key, parts)[block_of(target)]
    second = (block_of(target) + parts // 2) % parts
    return jnp.where((block_of(source) == near) | (block_of(source) == second), factor * drawn, drawn)


def block_levels(stream_key, shape, pieces, least, high):
    def one(position, parts):
        steps = jax.random.uniform(jax.random.fold_in(jax.random.fold_in(stream_key, 6), position), (parts,), jnp.float32, least / len(pieces), high / len(pieces))
        return jnp.repeat(jnp.exp(steps), shape[position] // parts).reshape((-1,) + (1,) * (len(shape) - position - 1))

    gain = one(*pieces[0])
    for cut in pieces[1:]:
        gain = gain * one(*cut)
    return gain


def shared_out(rng, own, number, rows, number_of, top, reach, lean):
    order = jax.random.permutation(rng, number_of)
    heavy_load, common = load_shares(number_of, rows * top, reach, lean, True), load_shares(number_of, rows * top, reach, lean, False)
    places = jnp.arange(number_of)

    def named(tallies, rotation):
        used = int((tallies > 0).sum())
        fixed = max(1, used // 4)
        shifted = fixed + (places - fixed + rotation * (used - fixed)) % max(1, number_of - fixed)
        return jnp.zeros((number_of,), jnp.int32).at[order[jnp.where(places < fixed, places, shifted)]].set(jnp.asarray(tallies, jnp.int32))

    tallies = jnp.where(number % 4 == 0, named(heavy_load, number // 4), named(common, number - number // 4 - 1))
    mixed = jax.random.permutation(jax.random.fold_in(own, 3), number_of)
    giver, taker = mixed[0:number_of // 2 * 2:2], mixed[1:number_of // 2 * 2:2]
    margin = jnp.minimum(tallies[giver] - 1, reach - tallies[taker]) // 2
    margin = jnp.where((giver == order[0]) | (taker == order[0]) | (tallies[taker] == 0), 0, jnp.maximum(margin, 0))
    shifted = jax.random.randint(jax.random.fold_in(own, 4), (number_of // 2,), 0, 1 << 20) % (margin + 1)
    tallies = tallies.at[giver].add(-shifted).at[taker].add(shifted)
    labels = jnp.searchsorted(jnp.cumsum(tallies), jnp.arange(rows * top), side="right").astype(jnp.int32)
    table = labels.reshape(top, rows).T
    table = table[jax.random.permutation(jax.random.fold_in(own, 1), rows)]
    rotation = jax.random.randint(jax.random.fold_in(own, 2), (rows, 1), 0, top)
    return jnp.take_along_axis(table, (jnp.arange(top)[None, :] + rotation) % top, axis=1)


def load_shares(count, total, bound, skew, full):
    portions = [(1 << 20) // math.isqrt(rank ** skew) + 1 for rank in range(1, count + 1)]
    largest = bound if full else min(bound, max(-(-total // count), total * portions[0] // sum(portions)))
    least = 1 if total - largest >= count - 1 else 0
    counts, surplus = [largest] + [least] * (count - 1), total - largest - least * (count - 1)
    while surplus > 0:
        candidates = [i for i in range(1, count) if counts[i] < largest] or [i for i in range(1, count) if counts[i] < bound]
        pool, budget = sum([portions[i] for i in candidates]), surplus
        for i in candidates:
            more = min(bound - counts[i], max(1, budget * portions[i] // pool), surplus)
            counts[i] = counts[i] + more
            surplus = surplus - more
    return np.array(counts)


def scatter_about(stream_key, dims, scale, limit, pieces=(), held_as=jnp.bfloat16):
    level = block_levels(stream_key, dims, pieces, -0.22, 0.18) if pieces else 1.0
    array = jax.random.normal(stream_key, dims, jnp.float32) * scale * level
    return jnp.minimum(jnp.maximum(array, -limit), limit).astype(held_as)


def bell_draw_with(key, dims, width, reach, cuts, heavy, kind=jnp.bfloat16):
    values = width * jax.random.normal(key, dims, jnp.float32)
    if cuts:
        values = values * block_levels(key, dims, cuts, -0.22, 0.18)
    return jnp.clip(with_spikes(values, jax.random.fold_in(key, 3), *heavy), -reach, reach).astype(kind)


def setup_inputs(seed: int = 0) -> dict:
    keys = jax.random.split(jax.random.key(seed), 7)
    tokens = bell_draw_with(keys[0], (TOKEN_TOTAL, MODEL_WIDTH), 1.0, 6.0, ((0, 16),), (0, 1, 16, 2.0))
    routes_keys = jax.random.split(jax.random.fold_in(keys[1], 1), TOKEN_TOTAL // GROUP_TOKENS)
    routes_turns = jax.random.permutation(jax.random.fold_in(keys[1], 3), TOKEN_TOTAL // GROUP_TOKENS)
    routes = jax.vmap(lambda own, number: shared_out(jax.random.fold_in(keys[1], 2), own, number, GROUP_TOKENS, ACTIVE_EXPERTS, TOKEN_EXPERTS, EXPERT_SLOTS, 2))(routes_keys, routes_turns).reshape((TOKEN_TOTAL, TOKEN_EXPERTS))
    gate_weight = scatter_about(keys[2], (ACTIVE_EXPERTS, MODEL_WIDTH, HIDDEN_UNITS), MODEL_WIDTH ** -0.5, 0.125, ((0, 4), (2, 2)))
    up_weight = scatter_about(keys[3], (ACTIVE_EXPERTS, MODEL_WIDTH, HIDDEN_UNITS), MODEL_WIDTH ** -0.5, 0.125, ((0, 4), (2, 2)))
    down_weight = scatter_about(keys[4], (ACTIVE_EXPERTS, HIDDEN_UNITS, MODEL_WIDTH), HIDDEN_UNITS ** -0.5, 0.21875, ((0, 4), (1, 2)))
    cotangent = scatter_about(keys[5], (ACTIVE_EXPERTS, EXPERT_ROWS, MODEL_WIDTH), 1.0, 6.0, ((0, 4), (1, 4)))
    return dict(tokens=tokens, routes=routes, gate_weight=gate_weight, up_weight=up_weight, down_weight=down_weight, cotangent=cotangent)


def expert_pass(packed):
    arrived, gate_matrix, up_matrix, down_matrix, upstream = packed
    gate_act = jnp.dot(arrived, gate_matrix, preferred_element_type=jnp.float32)
    up_act = jnp.dot(arrived, up_matrix, preferred_element_type=jnp.float32)
    sigmoid_gate = jax.nn.sigmoid(gate_act)
    silu_gate = gate_act * sigmoid_gate
    hidden = (silu_gate * up_act).astype(jnp.bfloat16)
    mixed = jnp.dot(hidden, down_matrix, preferred_element_type=jnp.float32).astype(jnp.bfloat16)
    dhidden = jnp.dot(upstream, down_matrix.T, preferred_element_type=jnp.float32)
    dgate = (dhidden * up_act * sigmoid_gate * (1.0 + gate_act * (1.0 - sigmoid_gate))).astype(jnp.bfloat16)
    dup = (dhidden * silu_gate).astype(jnp.bfloat16)
    slot_grad = (jnp.dot(dgate, gate_matrix.T, preferred_element_type=jnp.float32)
                 + jnp.dot(dup, up_matrix.T, preferred_element_type=jnp.float32)).astype(jnp.bfloat16)
    groups = N_DP
    arrived_groups = arrived.reshape(groups, -1, arrived.shape[1]).astype(jnp.float32)
    upstream_groups = upstream.reshape(groups, -1, upstream.shape[1]).astype(jnp.float32)
    hidden_groups = hidden.reshape(groups, -1, hidden.shape[1]).astype(jnp.float32)
    dgate_groups = dgate.reshape(groups, -1, dgate.shape[1]).astype(jnp.float32)
    dup_groups = dup.reshape(groups, -1, dup.shape[1]).astype(jnp.float32)
    part_gate = jnp.einsum("grd,grf->gdf", arrived_groups, dgate_groups)
    part_up = jnp.einsum("grd,grf->gdf", arrived_groups, dup_groups)
    part_down = jnp.einsum("grf,grd->gfd", hidden_groups, upstream_groups)
    grad_gate = jnp.sum(part_gate.astype(jnp.bfloat16).astype(jnp.float32), axis=0)
    grad_up = jnp.sum(part_up.astype(jnp.bfloat16).astype(jnp.float32), axis=0)
    grad_down = jnp.sum(part_down.astype(jnp.bfloat16).astype(jnp.float32), axis=0)
    return mixed, slot_grad, grad_gate, grad_up, grad_down


def reference(tokens, routes, gate_weight, up_weight, down_weight, cotangent):
    blocks = N_DP * N_EP
    feature_width = tokens.shape[1]
    flattened_routes = routes.reshape(blocks, GROUP_TOKENS * TOKEN_EXPERTS).astype(jnp.int32)
    one_hot_mask = (flattened_routes[:, :, None] == jnp.arange(ACTIVE_EXPERTS, dtype=jnp.int32)[None, None, :]).astype(jnp.int32)
    rank = jnp.cumsum(one_hot_mask, axis=1) - one_hot_mask
    slot_index = jnp.sum(rank * one_hot_mask, axis=2).astype(jnp.int32)
    block_ids = jnp.arange(blocks, dtype=jnp.int32)[:, None]
    group_ids = block_ids // N_EP
    source_ids = block_ids % N_EP
    destination = (flattened_routes * EXPERT_ROWS + group_ids * (N_EP * EXPERT_SLOTS) + source_ids * EXPERT_SLOTS + slot_index).astype(jnp.int32)
    replicated_rows = jnp.repeat(tokens, TOKEN_EXPERTS, axis=0)
    routed_tokens = jnp.zeros((ACTIVE_EXPERTS * EXPERT_ROWS, feature_width), jnp.bfloat16)
    routed_tokens = routed_tokens.at[destination.reshape(-1)].set(replicated_rows).reshape(ACTIVE_EXPERTS, EXPERT_ROWS, feature_width)
    mixed, slot_grad, grad_gate, grad_up, grad_down = lax.map(
        expert_pass, (routed_tokens, gate_weight, up_weight, down_weight, cotangent))
    return mixed, slot_grad, grad_gate, grad_up, grad_down
```

```python
import jax
import jax.numpy as jnp
from jax import lax
from jax.sharding import PartitionSpec as P

FIRST = (((0,), (0,)), ((), ()))
LAST = (((1,), (1,)), ((), ()))


def shift(index, step, count):
    return index ^ step if count & (count - 1) == 0 else (index + step) % count


def unshift(index, step, count):
    return index ^ step if count & (count - 1) == 0 else (index - step) % count


def send(value, axis, step):
    count = lax.axis_size(axis)
    return lax.ppermute(value, axis, [(at, shift(at, step, count)) for at in range(count)])


def in_order(blocks, index):
    count = len(blocks)
    if count & (count - 1):
        stacked = jnp.stack(blocks)
        return [stacked[(index - at) % count] for at in range(count)]
    bit = 1
    while bit < count:
        swap = (index & bit) != 0
        blocks = [jnp.where(swap, blocks[at ^ bit], blocks[at]) for at in range(count)]
        bit *= 2
    return blocks


def over_tp(value):
    steps = lax.axis_size("tp")
    return in_order([value] + [send(value, "tp", step) for step in range(1, steps)], lax.axis_index("tp"))


def columns_of(value, at, width):
    return lax.dynamic_slice_in_dim(value, at * width, width, axis=1)


def body(tokens, routes, gate_weight, up_weight, down_weight, cotangent):
    n_dp, n_ep, n_tp = (lax.axis_size(name) for name in ("dp", "ep", "tp"))
    mine_dp, mine_ep, mine_tp = (lax.axis_index(name) for name in ("dp", "ep", "tp"))
    tok_count, width = tokens.shape
    choices_each = routes.shape[1]
    pairs = tok_count * choices_each
    capacity = 2 * pairs // n_ep
    part = capacity // n_tp
    rows = n_ep * part
    hidden_units = gate_weight.shape[2]
    gate_matrix, up_matrix, down_matrix = gate_weight[0], up_weight[0], down_weight[0]
    block = width // n_dp

    upstream = cotangent[0].reshape(n_ep, n_tp, part, width).transpose(1, 0, 2, 3)
    up_mine = lax.dynamic_index_in_dim(upstream, mine_tp, 0, keepdims=False).reshape(rows, width)
    upstream = upstream.reshape(n_tp * rows, width)
    up_cols = [
        send(columns_of(up_mine, shift(mine_dp, step, n_dp), block), "dp", step) for step in range(1, n_dp)
    ]

    route = routes.reshape(1, pairs)
    named = route == jnp.arange(n_ep, dtype=jnp.int32)[:, None]
    earlier = jnp.arange(pairs)[:, None] < jnp.arange(pairs)[None, :]
    rank = jnp.dot(
        named.astype(jnp.bfloat16), earlier.astype(jnp.bfloat16), preferred_element_type=jnp.float32
    )
    slot = jnp.sum(jnp.where(named, rank, 0.0), axis=0, keepdims=True).astype(jnp.int32)
    step_of = unshift(route, mine_ep, n_ep)
    local = slot - mine_tp * part
    target = jnp.where((local >= 0) & (local < part), step_of * part + local, -1)
    placing = (jnp.arange(rows, dtype=jnp.int32)[:, None] == target).astype(jnp.bfloat16)
    packed = jnp.dot(
        placing, jnp.repeat(tokens, choices_each, axis=0), preferred_element_type=jnp.float32
    ).astype(jnp.bfloat16)
    got = [packed[:part]] + [
        send(packed[step * part:(step + 1) * part], "ep", step) for step in range(1, n_ep)
    ]
    arrived_mine = jnp.concatenate(in_order(got, mine_ep), axis=0)
    arrived = jnp.concatenate(over_tp(arrived_mine), axis=0)
    arr_cols = [
        send(columns_of(arrived_mine, shift(mine_dp, step, n_dp), block), "dp", step)
        for step in range(1, n_dp)
    ]

    gate_act = jnp.dot(arrived, gate_matrix, preferred_element_type=jnp.float32)
    up_act = jnp.dot(arrived, up_matrix, preferred_element_type=jnp.float32)
    dhidden = lax.dot_general(upstream, down_matrix, LAST, preferred_element_type=jnp.float32)
    sigmoid_gate = jax.nn.sigmoid(gate_act)
    silu_gate = gate_act * sigmoid_gate
    hidden = (silu_gate * up_act).astype(jnp.bfloat16)
    dgate = (dhidden * up_act * sigmoid_gate * (1.0 + gate_act * (1.0 - sigmoid_gate))).astype(
        jnp.bfloat16
    )
    dup = (dhidden * silu_gate).astype(jnp.bfloat16)
    units = jnp.concatenate([dgate, dup, hidden], axis=1)
    all_units = [units] + [send(units, "dp", step) for step in range(1, n_dp)]

    def over_cores(partial):
        half = partial.shape[1] // n_tp
        total = columns_of(partial, mine_tp, half)
        for step in range(1, n_tp):
            part_out = columns_of(partial, shift(mine_tp, step, n_tp), half)
            total = total + send(part_out.astype(jnp.bfloat16), "tp", step).astype(jnp.float32)
        total = total.astype(jnp.bfloat16).reshape(n_tp, n_ep, part, half)
        return total.transpose(1, 0, 2, 3).reshape(1, n_ep * capacity, half)

    mixed = over_cores(jnp.dot(hidden, down_matrix, preferred_element_type=jnp.float32))
    slot_grad = over_cores(
        lax.dot_general(dgate, gate_matrix, LAST, preferred_element_type=jnp.float32)
        + lax.dot_general(dup, up_matrix, LAST, preferred_element_type=jnp.float32)
    )

    def all_rows(own, cols):
        stacked = jnp.concatenate(cols, axis=1)
        both = jnp.concatenate(over_tp(stacked), axis=0)
        pieces = [columns_of(own, mine_dp, block)]
        pieces += [both[:, at * block:(at + 1) * block] for at in range(n_dp - 1)]
        return jnp.concatenate(pieces, axis=0)

    arr_all = all_rows(arrived, arr_cols)
    up_all = all_rows(upstream, up_cols)
    unit_all = jnp.concatenate(all_units, axis=0)
    grad_both = lax.dot_general(
        arr_all, unit_all[:, :2 * hidden_units], FIRST, preferred_element_type=jnp.float32
    )
    grad_down = lax.dot_general(
        unit_all[:, 2 * hidden_units:], up_all, FIRST, preferred_element_type=jnp.float32
    )
    return (
        mixed,
        slot_grad,
        grad_both[None, :, :hidden_units],
        grad_both[None, :, hidden_units:],
        grad_down[None],
    )


def solution(mesh):
    placed = (
        P(("dp", "ep"), None),
        P(("dp", "ep"), None),
        P("ep", None, "tp"),
        P("ep", None, "tp"),
        P("ep", "tp", None),
        P("ep", "dp", None),
    )
    return jax.shard_map(
        body,
        mesh=mesh,
        in_specs=placed,
        out_specs=(
            P("ep", "dp", "tp"),
            P("ep", "dp", "tp"),
            P("ep", "dp", "tp"),
            P("ep", "dp", "tp"),
            P("ep", "tp", "dp"),
        ),
        check_vma=False,
    )
```

```python
import jax
import jax.numpy as jnp
from jax import lax
from jax.experimental import pallas as pl
from jax.experimental.pallas import tpu as pltpu
from jax.sharding import PartitionSpec as P


FIRST = (((0,), (0,)), ((), ()))
LAST = (((1,), (1,)), ((), ()))


def shift(index, step, count):
    return index ^ step if count & (count - 1) == 0 else (index + step) % count


def unshift(index, step, count):
    return index ^ step if count & (count - 1) == 0 else (index - step) % count


def send(value, axis, step):
    count = lax.axis_size(axis)
    return lax.ppermute(value, axis, [(at, shift(at, step, count)) for at in range(count)])


def in_order(blocks, index):
    count = len(blocks)
    if count & (count - 1):
        stacked = jnp.stack(blocks)
        return [stacked[(index - at) % count] for at in range(count)]
    bit = 1
    while bit < count:
        swap = (index & bit) != 0
        blocks = [jnp.where(swap, blocks[at ^ bit], blocks[at]) for at in range(count)]
        bit *= 2
    return blocks


def over_tp(value):
    steps = lax.axis_size("tp")
    return in_order([value] + [send(value, "tp", step) for step in range(1, steps)], lax.axis_index("tp"))


def columns_of(value, at, width):
    return lax.dynamic_slice_in_dim(value, at * width, width, axis=1)


def call(kernel, outs, inputs, scratch=(), flops=0, grant=16, space=None):
    moved = sum(at.size * at.dtype.itemsize for at in (*inputs, *outs))
    return pl.pallas_call(
        kernel,
        out_shape=list(outs),
        in_specs=[pl.BlockSpec(memory_space=space or pltpu.VMEM)] * len(inputs),
        scratch_shapes=list(scratch),
        cost_estimate=pl.CostEstimate(flops=flops, bytes_accessed=moved, transcendentals=0),
        compiler_params=pltpu.CompilerParams(vmem_limit_bytes=grant << 20),
    )(*inputs)


def like(shape, dtype=jnp.bfloat16):
    return jax.ShapeDtypeStruct(shape, dtype)


def dot(left, right, dims=(((1,), (0,)), ((), ()))):
    return lax.dot_general(left, right, dims, preferred_element_type=jnp.float32)


def aligned(index, size):
    return pl.ds(pl.multiple_of(index * size, size), size)


def body(tokens, routes, gate_weight, up_weight, down_weight, cotangent):
    n_dp, n_ep, n_tp = (lax.axis_size(name) for name in ("dp", "ep", "tp"))
    tok_count, width = tokens.shape
    capacity = 2 * tok_count * routes.shape[1] // n_ep
    part = capacity // n_tp
    fits = (
        n_dp == 4 and n_tp == 2 and n_ep in (2, 4, 8, 16) and routes.shape[1] == 1
        and part % 16 == 0 and width % (128 * n_dp) == 0 and gate_weight.shape[2] % 128 == 0
    )
    chosen = blocked if fits else general
    return chosen(tokens, routes, gate_weight, up_weight, down_weight, cotangent)


def blocked(tokens, routes, gate_weight, up_weight, down_weight, cotangent):
    n_dp, n_ep, n_tp = (lax.axis_size(name) for name in ("dp", "ep", "tp"))
    tok_count, width = tokens.shape
    capacity = 2 * tok_count // n_ep
    part = capacity // n_tp
    rows = n_ep * part
    slots = n_ep * capacity
    units = gate_weight.shape[2]
    block = width // n_dp
    near = n_ep // 2
    chunk = near * capacity
    half = width // n_tp
    gate_matrix, up_matrix, down_matrix = gate_weight[0], up_weight[0], down_weight[0]
    upstream = cotangent[0]

    def pack(route_hbm, token_hbm, up_hbm, *refs):
        pieces, crossing = refs[:n_ep], refs[n_ep:n_ep + n_dp]
        route_ref, token_ref, packed, sems = refs[n_ep + n_dp:]
        at_dp, at_ep, at_tp = (lax.axis_index(name) for name in ("dp", "ep", "tp"))
        loads = [
            pltpu.make_async_copy(route_hbm, route_ref, sems.at[0]),
            pltpu.make_async_copy(token_hbm, token_ref, sems.at[1]),
        ]
        for step in range(n_dp):
            for source in range(n_ep):
                loads.append(
                    pltpu.make_async_copy(
                        up_hbm.at[
                            pl.ds(pl.multiple_of(source * capacity + at_tp * part, part), part),
                            aligned(at_dp ^ step, block),
                        ],
                        crossing[step].at[source * part:(source + 1) * part, :],
                        sems.at[len(loads)],
                    )
                )
        for load in loads:
            load.start()
        loads[0].wait()
        route = route_ref[...]
        named = route == lax.broadcasted_iota(jnp.int32, (16, tok_count), 0)
        earlier = lax.broadcasted_iota(jnp.int32, (tok_count, tok_count), 0) < lax.broadcasted_iota(
            jnp.int32, (tok_count, tok_count), 1
        )
        rank = dot(
            jnp.where(named, 1.0, 0.0).astype(jnp.bfloat16),
            jnp.where(earlier, 1.0, 0.0).astype(jnp.bfloat16),
        )
        slot = jnp.sum(jnp.where(named, rank, 0.0), axis=0, keepdims=True).astype(jnp.int32)
        local = slot - at_tp * part
        target = jnp.where((local >= 0) & (local < part), (route ^ at_ep) * part + local, -1)
        placing = lax.broadcasted_iota(jnp.int32, (rows, tok_count), 0) == target
        loads[1].wait()
        packed[...] = dot(
            jnp.where(placing, 1.0, 0.0).astype(jnp.bfloat16), token_ref[...]
        ).astype(jnp.bfloat16)
        for step in range(n_ep):
            pieces[step][...] = packed[step * part:(step + 1) * part, :]
        for step in range(n_dp):
            crossing[step][rows:, :] = packed[:, aligned(at_dp ^ step, block)]
        for load in loads[2:]:
            load.wait()

    packs = call(
        pack,
        [like((part, width))] * n_ep + [like((2 * rows, block))] * n_dp,
        tuple(
            pltpu.with_memory_space_constraint(at, pltpu.HBM)
            for at in (routes.reshape(1, tok_count), tokens, upstream)
        ),
        [
            pltpu.VMEM((1, tok_count), jnp.int32),
            pltpu.VMEM((tok_count, width), jnp.bfloat16),
            pltpu.VMEM((rows, width), jnp.bfloat16),
            pltpu.SemaphoreType.DMA((2 + n_dp * n_ep,)),
        ],
        2 * rows * tok_count * width,
        space=pltpu.HBM,
    )
    pieces, crossing = packs[:n_ep], packs[n_ep:]
    got = [pieces[0]] + [send(pieces[step], "ep", step) for step in range(1, n_ep)]
    crossed = [crossing[0]] + [send(crossing[step], "dp", step) for step in range(1, n_dp)]
    dhidden = dot(upstream, down_matrix, LAST)
    other = [send(piece, "tp", 1) for piece in got]

    def forward(number):
        def kernel(*refs):
            mine, theirs = refs[:near], refs[near:2 * near]
            dhidden_ref, gate_ref, up_ref, out_ref, arrived = refs[2 * near:]
            at_ep, at_tp = lax.axis_index("ep"), lax.axis_index("tp")
            for step in range(near):
                place = (at_ep % near) ^ step
                for ref, core in ((mine[step], at_tp), (theirs[step], 1 - at_tp)):
                    arrived[
                        pl.ds(pl.multiple_of(place * capacity + core * part, part), part), :
                    ] = ref[...]
            gate_act = dot(arrived[...], gate_ref[...])
            up_act = dot(arrived[...], up_ref[...])
            dhid = dhidden_ref[aligned((at_ep // near) ^ number, chunk), :]
            sigmoid_gate = jax.nn.sigmoid(gate_act)
            silu_gate = gate_act * sigmoid_gate
            out_ref[:, :units] = (
                dhid * up_act * sigmoid_gate * (1.0 + gate_act * (1.0 - sigmoid_gate))
            ).astype(jnp.bfloat16)
            out_ref[:, units:2 * units] = (dhid * silu_gate).astype(jnp.bfloat16)
            out_ref[:, 2 * units:] = (silu_gate * up_act).astype(jnp.bfloat16)

        chosen = range(number * near, (number + 1) * near)
        return call(
            kernel,
            [like((chunk, 3 * units))],
            (*(got[at] for at in chosen), *(other[at] for at in chosen), dhidden, gate_matrix, up_matrix),
            [pltpu.VMEM((chunk, width), jnp.bfloat16)],
            4 * chunk * width * units,
        )[0]

    first, second = forward(0), forward(1)
    x_first, y_first = send(first, "dp", 1), send(first, "dp", 2)
    x_second, y_second = send(second, "dp", 1), send(second, "dp", 2)
    far_first = send(y_first, "dp", 1)
    far_second = send(x_second, "dp", 2)

    def regroup(*refs):
        sources, outs, up_out = refs[:n_dp], refs[n_dp:n_dp + n_ep], refs[n_dp + n_ep]
        for group in range(n_dp):
            up_out[group * rows:(group + 1) * rows, :] = sources[group][:rows, :]
            for step in range(n_ep):
                outs[step][group * part:(group + 1) * part, :] = sources[group][
                    rows + step * part:rows + (step + 1) * part, :
                ]

    grouped = call(
        regroup, [like((n_dp * part, block))] * n_ep + [like((n_dp * rows, block))], crossed
    )
    up_half = grouped[n_ep]
    up_other = send(up_half, "tp", 1)
    cols = [grouped[0]] + [send(grouped[step], "ep", step) for step in range(1, n_ep)]
    cols_other = [send(piece, "tp", 1) for piece in cols]

    def outputs(first_ref, second_ref, gate_ref, up_ref, down_ref, sent_ref, mixed_ref, slot_ref):
        at_ep, at_tp = lax.axis_index("ep"), lax.axis_index("tp")
        for number, ref in enumerate((first_ref, second_ref)):
            place = (at_ep // near) ^ number
            at_rows = aligned(place, chunk)
            after = pl.ds(pl.multiple_of(slots + place * chunk, chunk), chunk)
            dgate, dup, hidden = (ref[:, at * units:(at + 1) * units] for at in range(3))
            for core, one, one_rows, two, two_rows in (
                (1 - at_tp, sent_ref, at_rows, sent_ref, after),
                (at_tp, mixed_ref, at_rows, slot_ref, at_rows),
            ):
                span = aligned(core, half)
                one[one_rows, :] = dot(hidden, down_ref[:, span]).astype(one.dtype)
                two[two_rows, :] = (
                    dot(dgate, gate_ref[span, :], LAST) + dot(dup, up_ref[span, :], LAST)
                ).astype(two.dtype)

    sent, mixed, slot_grad = call(
        outputs,
        [like((2 * slots, half))] + [like((slots, half), jnp.float32)] * 2,
        (first, second, gate_matrix, up_matrix, down_matrix),
        flops=6 * slots * width * units,
        grant=20,
    )
    came = send(sent, "tp", 1)

    def combine(came_ref, mixed_ref, slot_ref, mixed_out, slot_out):
        for at, kept, out in ((0, mixed_ref, mixed_out), (slots, slot_ref, slot_out)):
            other_part = came_ref[at:at + slots, :].astype(jnp.float32)
            out[...] = (kept[...] + other_part).astype(jnp.bfloat16)

    mixed, slot_grad = call(combine, [like((slots, half))] * 2, (came, mixed, slot_grad))

    def gather(*refs):
        mine, theirs = refs[:n_ep], refs[n_ep:2 * n_ep]
        up_mine, up_theirs, left, right = refs[2 * n_ep:]
        at_ep, at_tp = lax.axis_index("ep"), lax.axis_index("tp")
        for group in range(n_dp):
            for step in range(n_ep):
                for core, col_ref, up_ref in (
                    (at_tp, mine[step], up_mine), (1 - at_tp, theirs[step], up_theirs)
                ):
                    start = group * slots + (at_ep ^ step) * capacity + core * part
                    left[pl.ds(pl.multiple_of(start, part), part), :] = col_ref[
                        group * part:(group + 1) * part, :
                    ]
                    start = group * slots + step * capacity + core * part
                    right[pl.ds(pl.multiple_of(start, part), part), :] = up_ref[
                        group * rows + step * part:group * rows + (step + 1) * part, :
                    ]

    every = n_dp * slots
    left, right = call(gather, [like((every, block))] * 2, (*cols, *cols_other, up_half, up_other))
    last = n_dp - 1

    near_rows = last * slots

    def early(*refs):
        firsts, seconds = refs[:last], refs[last:2 * last]
        left_ref, right_ref, gate_out, up_out, down_out, both = refs[2 * last:]
        at_ep = lax.axis_index("ep")
        for group in range(last):
            for number, ref in ((0, firsts[group]), (1, seconds[group])):
                place = (at_ep // near) ^ number
                both[pl.ds(pl.multiple_of(group * slots + place * chunk, chunk), chunk), :] = ref[...]
        grads = dot(left_ref[:near_rows, :], both[:, :2 * units], FIRST)
        gate_out[...] = grads[:, :units]
        up_out[...] = grads[:, units:]
        down_out[...] = dot(both[:, 2 * units:], right_ref[:near_rows, :], FIRST)

    shapes = [like((block, units), jnp.float32)] * 2 + [like((units, block), jnp.float32)]
    sums = call(
        early,
        shapes,
        (first, x_first, y_first, second, x_second, y_second, left, right),
        [pltpu.VMEM((near_rows, 3 * units), jnp.bfloat16)],
        6 * near_rows * block * units,
        20,
    )

    def late(first_ref, second_ref, left_ref, right_ref, gate_in, up_in, down_in, *refs):
        gate_out, up_out, down_out, both = refs
        at_ep = lax.axis_index("ep")
        for number, ref in ((0, first_ref), (1, second_ref)):
            both[aligned((at_ep // near) ^ number, chunk), :] = ref[...]
        grads = dot(left_ref[near_rows:, :], both[:, :2 * units], FIRST)
        gate_out[...] = gate_in[...] + grads[:, :units]
        up_out[...] = up_in[...] + grads[:, units:]
        down_out[...] = down_in[...] + dot(both[:, 2 * units:], right_ref[near_rows:, :], FIRST)

    grads = call(
        late,
        shapes,
        (far_first, far_second, left, right, *sums),
        [pltpu.VMEM((slots, 3 * units), jnp.bfloat16)],
        6 * slots * block * units,
    )
    return (mixed[None], slot_grad[None], *(grad[None] for grad in grads))


def general(tokens, routes, gate_weight, up_weight, down_weight, cotangent):
    n_dp, n_ep, n_tp = (lax.axis_size(name) for name in ("dp", "ep", "tp"))
    mine_dp, mine_ep, mine_tp = (lax.axis_index(name) for name in ("dp", "ep", "tp"))
    tok_count, width = tokens.shape
    choices_each = routes.shape[1]
    pairs = tok_count * choices_each
    capacity = 2 * pairs // n_ep
    part = capacity // n_tp
    rows = n_ep * part
    hidden_units = gate_weight.shape[2]
    gate_matrix, up_matrix, down_matrix = gate_weight[0], up_weight[0], down_weight[0]
    block = width // n_dp

    upstream = cotangent[0].reshape(n_ep, n_tp, part, width).transpose(1, 0, 2, 3)
    up_mine = lax.dynamic_index_in_dim(upstream, mine_tp, 0, keepdims=False).reshape(rows, width)
    upstream = upstream.reshape(n_tp * rows, width)
    up_cols = [
        send(columns_of(up_mine, shift(mine_dp, step, n_dp), block), "dp", step) for step in range(1, n_dp)
    ]

    route = routes.reshape(1, pairs)
    named = route == jnp.arange(n_ep, dtype=jnp.int32)[:, None]
    earlier = jnp.arange(pairs)[:, None] < jnp.arange(pairs)[None, :]
    rank = jnp.dot(
        named.astype(jnp.bfloat16), earlier.astype(jnp.bfloat16), preferred_element_type=jnp.float32
    )
    slot = jnp.sum(jnp.where(named, rank, 0.0), axis=0, keepdims=True).astype(jnp.int32)
    step_of = unshift(route, mine_ep, n_ep)
    local = slot - mine_tp * part
    target = jnp.where((local >= 0) & (local < part), step_of * part + local, -1)
    placing = (jnp.arange(rows, dtype=jnp.int32)[:, None] == target).astype(jnp.bfloat16)
    packed = jnp.dot(
        placing, jnp.repeat(tokens, choices_each, axis=0), preferred_element_type=jnp.float32
    ).astype(jnp.bfloat16)
    got = [packed[:part]] + [
        send(packed[step * part:(step + 1) * part], "ep", step) for step in range(1, n_ep)
    ]
    arrived_mine = jnp.concatenate(in_order(got, mine_ep), axis=0)
    arrived = jnp.concatenate(over_tp(arrived_mine), axis=0)
    arr_cols = [
        send(columns_of(arrived_mine, shift(mine_dp, step, n_dp), block), "dp", step)
        for step in range(1, n_dp)
    ]

    gate_act = jnp.dot(arrived, gate_matrix, preferred_element_type=jnp.float32)
    up_act = jnp.dot(arrived, up_matrix, preferred_element_type=jnp.float32)
    dhidden = lax.dot_general(upstream, down_matrix, LAST, preferred_element_type=jnp.float32)
    sigmoid_gate = jax.nn.sigmoid(gate_act)
    silu_gate = gate_act * sigmoid_gate
    hidden = (silu_gate * up_act).astype(jnp.bfloat16)
    dgate = (dhidden * up_act * sigmoid_gate * (1.0 + gate_act * (1.0 - sigmoid_gate))).astype(
        jnp.bfloat16
    )
    dup = (dhidden * silu_gate).astype(jnp.bfloat16)
    units = jnp.concatenate([dgate, dup, hidden], axis=1)
    all_units = [units] + [send(units, "dp", step) for step in range(1, n_dp)]

    def over_cores(partial):
        half = partial.shape[1] // n_tp
        total = columns_of(partial, mine_tp, half)
        for step in range(1, n_tp):
            part_out = columns_of(partial, shift(mine_tp, step, n_tp), half)
            total = total + send(part_out.astype(jnp.bfloat16), "tp", step).astype(jnp.float32)
        total = total.astype(jnp.bfloat16).reshape(n_tp, n_ep, part, half)
        return total.transpose(1, 0, 2, 3).reshape(1, n_ep * capacity, half)

    mixed = over_cores(jnp.dot(hidden, down_matrix, preferred_element_type=jnp.float32))
    slot_grad = over_cores(
        lax.dot_general(dgate, gate_matrix, LAST, preferred_element_type=jnp.float32)
        + lax.dot_general(dup, up_matrix, LAST, preferred_element_type=jnp.float32)
    )

    def all_rows(own, cols):
        stacked = jnp.concatenate(cols, axis=1)
        both = jnp.concatenate(over_tp(stacked), axis=0)
        pieces = [columns_of(own, mine_dp, block)]
        pieces += [both[:, at * block:(at + 1) * block] for at in range(n_dp - 1)]
        return jnp.concatenate(pieces, axis=0)

    arr_all = all_rows(arrived, arr_cols)
    up_all = all_rows(upstream, up_cols)
    unit_all = jnp.concatenate(all_units, axis=0)
    grad_both = lax.dot_general(
        arr_all, unit_all[:, :2 * hidden_units], FIRST, preferred_element_type=jnp.float32
    )
    grad_down = lax.dot_general(
        unit_all[:, 2 * hidden_units:], up_all, FIRST, preferred_element_type=jnp.float32
    )
    return (
        mixed,
        slot_grad,
        grad_both[None, :, :hidden_units],
        grad_both[None, :, hidden_units:],
        grad_down[None],
    )


def solution(mesh):
    placed = (
        P(("dp", "ep"), None),
        P(("dp", "ep"), None),
        P("ep", None, "tp"),
        P("ep", None, "tp"),
        P("ep", "tp", None),
        P("ep", "dp", None),
    )
    return jax.shard_map(
        body,
        mesh=mesh,
        in_specs=placed,
        out_specs=(
            P("ep", "dp", "tp"),
            P("ep", "dp", "tp"),
            P("ep", "dp", "tp"),
            P("ep", "dp", "tp"),
            P("ep", "tp", "dp"),
        ),
        check_vma=False,
    )
```

```python
import jax
import jax.numpy as jnp
from jax import lax
from jax.experimental import pallas as pl
from jax.experimental.pallas import tpu as pltpu
from jax.sharding import PartitionSpec as P


FIRST = (((0,), (0,)), ((), ()))
LAST = (((1,), (1,)), ((), ()))


def shift(index, step, count):
    return index ^ step if count & (count - 1) == 0 else (index + step) % count


def unshift(index, step, count):
    return index ^ step if count & (count - 1) == 0 else (index - step) % count


def send(value, axis, step):
    count = lax.axis_size(axis)
    return lax.ppermute(value, axis, [(at, shift(at, step, count)) for at in range(count)])


def in_order(blocks, index):
    count = len(blocks)
    if count & (count - 1):
        stacked = jnp.stack(blocks)
        return [stacked[(index - at) % count] for at in range(count)]
    bit = 1
    while bit < count:
        swap = (index & bit) != 0
        blocks = [jnp.where(swap, blocks[at ^ bit], blocks[at]) for at in range(count)]
        bit *= 2
    return blocks


def over_tp(value):
    steps = lax.axis_size("tp")
    return in_order([value] + [send(value, "tp", step) for step in range(1, steps)], lax.axis_index("tp"))


def columns_of(value, at, width):
    return lax.dynamic_slice_in_dim(value, at * width, width, axis=1)


def call(kernel, outs, inputs, scratch=(), flops=0, grant=16, space=None, out_space=None):
    moved = sum(at.size * at.dtype.itemsize for at in (*inputs, *outs))
    return pl.pallas_call(
        kernel,
        out_shape=list(outs),
        in_specs=[pl.BlockSpec(memory_space=space or pltpu.VMEM)] * len(inputs),
        out_specs=[pl.BlockSpec(memory_space=out_space or pltpu.VMEM)] * len(outs),
        scratch_shapes=list(scratch),
        cost_estimate=pl.CostEstimate(flops=flops, bytes_accessed=moved, transcendentals=0),
        compiler_params=pltpu.CompilerParams(vmem_limit_bytes=grant << 20),
    )(*inputs)


def like(shape, dtype=jnp.bfloat16):
    return jax.ShapeDtypeStruct(shape, dtype)


def dot(left, right, dims=(((1,), (0,)), ((), ()))):
    return lax.dot_general(left, right, dims, preferred_element_type=jnp.float32)


def aligned(index, size):
    return pl.ds(pl.multiple_of(index * size, size), size)


def body(tokens, routes, gate_weight, up_weight, down_weight, cotangent):
    n_dp, n_ep, n_tp = (lax.axis_size(name) for name in ("dp", "ep", "tp"))
    tok_count, width = tokens.shape
    capacity = 2 * tok_count * routes.shape[1] // n_ep
    part = capacity // n_tp
    fits = (
        n_dp == 4 and n_tp == 2 and n_ep in (2, 4, 8, 16) and routes.shape[1] == 1
        and part % 16 == 0 and width % (128 * n_dp) == 0 and gate_weight.shape[2] % 128 == 0
    )
    chosen = blocked if fits else general
    return chosen(tokens, routes, gate_weight, up_weight, down_weight, cotangent)


def blocked(tokens, routes, gate_weight, up_weight, down_weight, cotangent):
    n_dp, n_ep, n_tp = (lax.axis_size(name) for name in ("dp", "ep", "tp"))
    tok_count, width = tokens.shape
    capacity = 2 * tok_count // n_ep
    part = capacity // n_tp
    rows = n_ep * part
    slots = n_ep * capacity
    units = gate_weight.shape[2]
    block = width // n_dp
    near = n_ep // 2
    chunk = near * capacity
    half = width // n_tp
    gate_matrix, up_matrix, down_matrix = gate_weight[0], up_weight[0], down_weight[0]
    upstream = cotangent[0]

    def pack(route_hbm, token_hbm, up_hbm, *refs):
        pieces, crossing = refs[:n_ep], refs[n_ep:n_ep + n_dp]
        route_ref, token_ref, packed, sems = refs[n_ep + n_dp:]
        at_dp, at_ep, at_tp = (lax.axis_index(name) for name in ("dp", "ep", "tp"))
        loads = [
            pltpu.make_async_copy(route_hbm, route_ref, sems.at[0]),
            pltpu.make_async_copy(token_hbm, token_ref, sems.at[1]),
        ]
        for step in range(n_dp):
            for source in range(n_ep):
                loads.append(
                    pltpu.make_async_copy(
                        up_hbm.at[
                            pl.ds(pl.multiple_of(source * capacity + at_tp * part, part), part),
                            aligned(at_dp ^ step, block),
                        ],
                        crossing[step].at[source * part:(source + 1) * part, :],
                        sems.at[len(loads)],
                    )
                )
        for load in loads:
            load.start()
        loads[0].wait()
        route = route_ref[...]
        named = route == lax.broadcasted_iota(jnp.int32, (16, tok_count), 0)
        earlier = lax.broadcasted_iota(jnp.int32, (tok_count, tok_count), 0) < lax.broadcasted_iota(
            jnp.int32, (tok_count, tok_count), 1
        )
        rank = dot(
            jnp.where(named, 1.0, 0.0).astype(jnp.bfloat16),
            jnp.where(earlier, 1.0, 0.0).astype(jnp.bfloat16),
        )
        slot = jnp.sum(jnp.where(named, rank, 0.0), axis=0, keepdims=True).astype(jnp.int32)
        local = slot - at_tp * part
        target = jnp.where((local >= 0) & (local < part), (route ^ at_ep) * part + local, -1)
        placing = lax.broadcasted_iota(jnp.int32, (rows, tok_count), 0) == target
        loads[1].wait()
        packed[...] = dot(
            jnp.where(placing, 1.0, 0.0).astype(jnp.bfloat16), token_ref[...]
        ).astype(jnp.bfloat16)
        for step in range(n_ep):
            pieces[step][...] = packed[step * part:(step + 1) * part, :]
        for step in range(n_dp):
            crossing[step][rows:, :] = packed[:, aligned(at_dp ^ step, block)]
        for load in loads[2:]:
            load.wait()

    packs = call(
        pack,
        [like((part, width))] * n_ep + [like((2 * rows, block))] * n_dp,
        tuple(
            pltpu.with_memory_space_constraint(at, pltpu.HBM)
            for at in (routes.reshape(1, tok_count), tokens, upstream)
        ),
        [
            pltpu.VMEM((1, tok_count), jnp.int32),
            pltpu.VMEM((tok_count, width), jnp.bfloat16),
            pltpu.VMEM((rows, width), jnp.bfloat16),
            pltpu.SemaphoreType.DMA((2 + n_dp * n_ep,)),
        ],
        2 * rows * tok_count * width,
        space=pltpu.HBM,
    )
    pieces, crossing = packs[:n_ep], packs[n_ep:]
    got = [pieces[0]] + [send(pieces[step], "ep", step) for step in range(1, n_ep)]
    crossed = [crossing[0]] + [send(crossing[step], "dp", step) for step in range(1, n_dp)]
    dhidden = dot(upstream, down_matrix, LAST)
    other = [send(piece, "tp", 1) for piece in got]

    def forward(number):
        def kernel(*refs):
            mine, theirs = refs[:near], refs[near:2 * near]
            dhidden_ref, gate_ref, up_ref, out_ref, arrived = refs[2 * near:]
            at_ep, at_tp = lax.axis_index("ep"), lax.axis_index("tp")
            for step in range(near):
                place = (at_ep % near) ^ step
                for ref, core in ((mine[step], at_tp), (theirs[step], 1 - at_tp)):
                    arrived[
                        pl.ds(pl.multiple_of(place * capacity + core * part, part), part), :
                    ] = ref[...]
            gate_act = dot(arrived[...], gate_ref[...])
            up_act = dot(arrived[...], up_ref[...])
            dhid = dhidden_ref[aligned((at_ep // near) ^ number, chunk), :]
            sigmoid_gate = jax.nn.sigmoid(gate_act)
            silu_gate = gate_act * sigmoid_gate
            dgate = dhid * up_act * sigmoid_gate * (1.0 + gate_act * (1.0 - sigmoid_gate))
            for at, value in enumerate((dgate, dhid * silu_gate, silu_gate * up_act)):
                out_ref[:, at * units:(at + 1) * units] = value.astype(jnp.bfloat16)

        chosen = range(number * near, (number + 1) * near)
        return call(
            kernel,
            [like((chunk, 3 * units))],
            (*(got[at] for at in chosen), *(other[at] for at in chosen), dhidden, gate_matrix, up_matrix),
            [pltpu.VMEM((chunk, width), jnp.bfloat16)],
            4 * chunk * width * units,
        )

    (first,), (second,) = forward(0), forward(1)
    x_first, y_first = send(first, "dp", 1), send(first, "dp", 2)
    x_second, y_second = send(second, "dp", 1), send(second, "dp", 2)
    far_first = send(y_first, "dp", 1)
    far_second = send(x_second, "dp", 2)

    def regroup(*refs):
        sources, outs, up_out = refs[:n_dp], refs[n_dp:n_dp + n_ep], refs[n_dp + n_ep]
        for group in range(n_dp):
            up_out[group * rows:(group + 1) * rows, :] = sources[group][:rows, :]
            for step in range(n_ep):
                outs[step][group * part:(group + 1) * part, :] = sources[group][
                    rows + step * part:rows + (step + 1) * part, :
                ]

    grouped = call(
        regroup, [like((n_dp * part, block))] * n_ep + [like((n_dp * rows, block))], crossed
    )
    up_half = grouped[n_ep]
    up_other = send(up_half, "tp", 1)
    cols = [grouped[0]] + [send(grouped[step], "ep", step) for step in range(1, n_ep)]
    cols_other = [send(piece, "tp", 1) for piece in cols]

    def outputs(unit_ref, gate_ref, up_ref, down_ref, sent_ref, mixed_ref, slot_ref):
        at_tp = lax.axis_index("tp")
        dgate, dup, hidden = (unit_ref[:, at * units:(at + 1) * units] for at in range(3))
        for core, one, two in (
            (1 - at_tp, sent_ref.at[:chunk, :], sent_ref.at[chunk:, :]), (at_tp, mixed_ref, slot_ref)
        ):
            span = aligned(core, half)
            one[...] = dot(hidden, down_ref[:, span]).astype(one.dtype)
            two[...] = (
                dot(dgate, gate_ref[span, :], LAST) + dot(dup, up_ref[span, :], LAST)
            ).astype(two.dtype)

    kept, came = [], []
    for unit in (first, second):
        sent, *own = call(
            outputs,
            [like((2 * chunk, half))] + [like((chunk, half), jnp.float32)] * 2,
            (unit, gate_matrix, up_matrix, down_matrix),
            flops=6 * chunk * width * units,
        )
        kept += own
        came.append(send(sent, "tp", 1))

    def combine(*refs):
        mixed_out, slot_out = refs[6:]
        for number in range(2):
            at_rows = aligned((lax.axis_index("ep") // near) ^ number, chunk)
            for at, kept_ref, out in (
                (0, refs[2 + 2 * number], mixed_out), (chunk, refs[3 + 2 * number], slot_out)
            ):
                other_part = refs[number][at:at + chunk, :].astype(jnp.float32)
                out[at_rows, :] = (kept_ref[...] + other_part).astype(jnp.bfloat16)

    mixed, slot_grad = call(combine, [like((slots, half))] * 2, (*came, *kept))
    last = n_dp - 1
    every = n_dp * chunk
    cores = lambda: ((0, lax.axis_index("tp")), (1, 1 - lax.axis_index("tp")))

    def set_left(left, refs, groups, at=0):
        for index, group in enumerate(groups):
            for step in range(near):
                place = (lax.axis_index("ep") % near) ^ step
                for which, core in cores():
                    start = at + index * chunk + place * capacity + core * part
                    left[pl.ds(pl.multiple_of(start, part), part), :] = refs[which * near + step][
                        group * part:(group + 1) * part, :
                    ]

    def set_right(right, at, refs, group, number):
        first_source = ((lax.axis_index("ep") // near) ^ number) * near
        for source in range(near):
            for which, core in cores():
                start = at + source * capacity + core * part
                taken = group * rows + (first_source + source) * part
                right[pl.ds(pl.multiple_of(start, part), part), :] = refs[which][
                    pl.ds(pl.multiple_of(taken, part), part), :
                ]

    def early(*refs):
        firsts, seconds, refs = refs[:last], refs[last:2 * last], refs[2 * last:]
        pieces, ups = refs[:2 * near], refs[2 * near:2 * near + 2]
        gate_out, up_out, down_out, left, right, both, hid = refs[2 * near + 2:]
        set_left(left, pieces, range(last))
        for group in range(last):
            span = slice(group * chunk, (group + 1) * chunk)
            both[span, :] = firsts[group][:, :2 * units]
            hid[span, :] = firsts[group][:, 2 * units:]
            set_right(right, group * chunk, ups, group, 0)
        for group in range(last):
            hid[known + group * chunk:known + (group + 1) * chunk, :] = seconds[group][:, 2 * units:]
            set_right(right, known + group * chunk, ups, group, 1)
        grads = dot(left[...], both[...], FIRST)
        gate_out[...] = grads[:, :units]
        up_out[...] = grads[:, units:]
        down_out[...] = dot(hid[...], right[...], FIRST)

    shapes = [like((block, units), jnp.float32)] * 2 + [like((units, block), jnp.float32)]
    ups = (up_half, up_other)
    known = last * chunk
    sums = call(
        early,
        shapes,
        (
            first, x_first, y_first, second, x_second, y_second,
            *cols[:near], *cols_other[:near], *ups,
        ),
        [
            pltpu.VMEM((known, block), jnp.bfloat16),
            pltpu.VMEM((2 * known, block), jnp.bfloat16),
            pltpu.VMEM((known, 2 * units), jnp.bfloat16),
            pltpu.VMEM((2 * known, units), jnp.bfloat16),
        ],
        8 * known * block * units,
    )

    def final(*refs):
        arrays, refs = refs[:n_dp + 1], refs[n_dp + 1:]
        pieces, ups, refs = refs[:4 * near], refs[4 * near:4 * near + 2], refs[4 * near + 2:]
        gate_in, up_in, down_in, gate_hbm, up_hbm, down_hbm, *scratch = refs
        gate_out, up_out, down_out, left, right, gates, dups, hid, sems = scratch
        set_left(left, pieces[2 * near:], range(n_dp))
        set_left(left, pieces[:2 * near], (last,), every)
        for number in range(2):
            set_right(right, number * chunk, ups, last, number)
        hid[:chunk, :] = arrays[n_dp][:, 2 * units:]
        hid[chunk:, :] = arrays[last][:, 2 * units:]
        down_out[...] = down_in[...] + dot(hid[...], right[...], FIRST)
        down_copy = pltpu.make_async_copy(down_out, down_hbm, sems.at[0])
        down_copy.start()
        for at, ref in enumerate(arrays):
            dups[at * chunk:(at + 1) * chunk, :] = ref[:, units:2 * units]
        up_out[...] = up_in[...] + dot(left[...], dups[...], FIRST)
        up_copy = pltpu.make_async_copy(up_out, up_hbm, sems.at[1])
        up_copy.start()
        for at, ref in enumerate(arrays):
            gates[at * chunk:(at + 1) * chunk, :] = ref[:, :units]
        copies = [down_copy, up_copy]
        for number in range(2):
            span = slice(number * block // 2, (number + 1) * block // 2)
            gate_out[span, :] = gate_in[span, :] + dot(left[:, span], gates[...], FIRST)
            copies.append(
                pltpu.make_async_copy(gate_out.at[span, :], gate_hbm.at[span, :], sems.at[2 + number])
            )
            copies[-1].start()
        for copy in copies:
            copy.wait()

    grad_gate, grad_up, grad_down = call(
        final,
        shapes,
        (
            second, x_second, y_second, far_second, far_first,
            *cols[:near], *cols_other[:near], *cols[near:], *cols_other[near:], *ups, *sums,
        ),
        [
            *(pltpu.VMEM(shape.shape, jnp.float32) for shape in shapes),
            pltpu.VMEM((every + chunk, block), jnp.bfloat16),
            pltpu.VMEM((2 * chunk, block), jnp.bfloat16),
            pltpu.VMEM((every + chunk, units), jnp.bfloat16),
            pltpu.VMEM((every + chunk, units), jnp.bfloat16),
            pltpu.VMEM((2 * chunk, units), jnp.bfloat16),
            pltpu.SemaphoreType.DMA((4,)),
        ],
        4 * (every + 2 * chunk) * block * units,
        out_space=pltpu.HBM,
    )
    return (mixed[None], slot_grad[None], grad_gate[None], grad_up[None], grad_down[None])


def general(tokens, routes, gate_weight, up_weight, down_weight, cotangent):
    n_dp, n_ep, n_tp = (lax.axis_size(name) for name in ("dp", "ep", "tp"))
    mine_dp, mine_ep, mine_tp = (lax.axis_index(name) for name in ("dp", "ep", "tp"))
    tok_count, width = tokens.shape
    choices_each = routes.shape[1]
    pairs = tok_count * choices_each
    capacity = 2 * pairs // n_ep
    part = capacity // n_tp
    rows = n_ep * part
    hidden_units = gate_weight.shape[2]
    gate_matrix, up_matrix, down_matrix = gate_weight[0], up_weight[0], down_weight[0]
    block = width // n_dp

    upstream = cotangent[0].reshape(n_ep, n_tp, part, width).transpose(1, 0, 2, 3)
    up_mine = lax.dynamic_index_in_dim(upstream, mine_tp, 0, keepdims=False).reshape(rows, width)
    upstream = upstream.reshape(n_tp * rows, width)
    up_cols = [
        send(columns_of(up_mine, shift(mine_dp, step, n_dp), block), "dp", step) for step in range(1, n_dp)
    ]

    route = routes.reshape(1, pairs)
    named = route == jnp.arange(n_ep, dtype=jnp.int32)[:, None]
    earlier = jnp.arange(pairs)[:, None] < jnp.arange(pairs)[None, :]
    rank = jnp.dot(
        named.astype(jnp.bfloat16), earlier.astype(jnp.bfloat16), preferred_element_type=jnp.float32
    )
    slot = jnp.sum(jnp.where(named, rank, 0.0), axis=0, keepdims=True).astype(jnp.int32)
    step_of = unshift(route, mine_ep, n_ep)
    local = slot - mine_tp * part
    target = jnp.where((local >= 0) & (local < part), step_of * part + local, -1)
    placing = (jnp.arange(rows, dtype=jnp.int32)[:, None] == target).astype(jnp.bfloat16)
    packed = jnp.dot(
        placing, jnp.repeat(tokens, choices_each, axis=0), preferred_element_type=jnp.float32
    ).astype(jnp.bfloat16)
    got = [packed[:part]] + [
        send(packed[step * part:(step + 1) * part], "ep", step) for step in range(1, n_ep)
    ]
    arrived_mine = jnp.concatenate(in_order(got, mine_ep), axis=0)
    arrived = jnp.concatenate(over_tp(arrived_mine), axis=0)
    arr_cols = [
        send(columns_of(arrived_mine, shift(mine_dp, step, n_dp), block), "dp", step)
        for step in range(1, n_dp)
    ]

    gate_act = jnp.dot(arrived, gate_matrix, preferred_element_type=jnp.float32)
    up_act = jnp.dot(arrived, up_matrix, preferred_element_type=jnp.float32)
    dhidden = lax.dot_general(upstream, down_matrix, LAST, preferred_element_type=jnp.float32)
    sigmoid_gate = jax.nn.sigmoid(gate_act)
    silu_gate = gate_act * sigmoid_gate
    hidden = (silu_gate * up_act).astype(jnp.bfloat16)
    dgate = (dhidden * up_act * sigmoid_gate * (1.0 + gate_act * (1.0 - sigmoid_gate))).astype(
        jnp.bfloat16
    )
    dup = (dhidden * silu_gate).astype(jnp.bfloat16)
    units = jnp.concatenate([dgate, dup, hidden], axis=1)
    all_units = [units] + [send(units, "dp", step) for step in range(1, n_dp)]

    def over_cores(partial):
        half = partial.shape[1] // n_tp
        total = columns_of(partial, mine_tp, half)
        for step in range(1, n_tp):
            part_out = columns_of(partial, shift(mine_tp, step, n_tp), half)
            total = total + send(part_out.astype(jnp.bfloat16), "tp", step).astype(jnp.float32)
        total = total.astype(jnp.bfloat16).reshape(n_tp, n_ep, part, half)
        return total.transpose(1, 0, 2, 3).reshape(1, n_ep * capacity, half)

    mixed = over_cores(jnp.dot(hidden, down_matrix, preferred_element_type=jnp.float32))
    slot_grad = over_cores(
        lax.dot_general(dgate, gate_matrix, LAST, preferred_element_type=jnp.float32)
        + lax.dot_general(dup, up_matrix, LAST, preferred_element_type=jnp.float32)
    )

    def all_rows(own, cols):
        stacked = jnp.concatenate(cols, axis=1)
        both = jnp.concatenate(over_tp(stacked), axis=0)
        pieces = [columns_of(own, mine_dp, block)]
        pieces += [both[:, at * block:(at + 1) * block] for at in range(n_dp - 1)]
        return jnp.concatenate(pieces, axis=0)

    arr_all = all_rows(arrived, arr_cols)
    up_all = all_rows(upstream, up_cols)
    unit_all = jnp.concatenate(all_units, axis=0)
    grad_both = lax.dot_general(
        arr_all, unit_all[:, :2 * hidden_units], FIRST, preferred_element_type=jnp.float32
    )
    grad_down = lax.dot_general(
        unit_all[:, 2 * hidden_units:], up_all, FIRST, preferred_element_type=jnp.float32
    )
    return (
        mixed,
        slot_grad,
        grad_both[None, :, :hidden_units],
        grad_both[None, :, hidden_units:],
        grad_down[None],
    )


def solution(mesh):
    placed = (
        P(("dp", "ep"), None),
        P(("dp", "ep"), None),
        P("ep", None, "tp"),
        P("ep", None, "tp"),
        P("ep", "tp", None),
        P("ep", "dp", None),
    )
    return jax.shard_map(
        body,
        mesh=mesh,
        in_specs=placed,
        out_specs=(
            P("ep", "dp", "tp"),
            P("ep", "dp", "tp"),
            P("ep", "dp", "tp"),
            P("ep", "dp", "tp"),
            P("ep", "tp", "dp"),
        ),
        check_vma=False,
    )
```
